32 devices in a mesh: ctx: 8 (over y, x, core), chan: 4 (over z).
Axes of the slice: x: 2, y: 2, z: 4, core: 2. Of those that a mesh axis runs over, the one named last changes fastest.
Arguments:
- signal: float32 [2048, 2048], P('chan', 'ctx'), may hold values from -6 to 6
- gate_in: float32 [2048, 2048], P('chan', 'ctx'), may hold values from -6 to 6
- filter_raw: float32 [2048, 2048], P('chan', 'ctx'), may hold values from -6 to 6
- short_kernel: float32 [2048, 7], P('chan'), may hold values from -2 to 2
- skip_gain: float32 [2048], P('chan'), may hold values from -4 to 4
- out_weight: float32 [2048, 2048], P(None, 'chan'), may hold values from -0.125 to 0.125
- cotangent: float32 [2048, 2048], P('chan', 'ctx'), may hold values from -6 to 6
Outputs:
- grad_gate: float32 [2048, 2048], P('chan', 'ctx')
- grad_signal: float32 [2048, 2048], P('chan', 'ctx')
- grad_filter: float32 [2048, 2048], P('chan', 'ctx')
- grad_kernel: float32 [2048, 7], P('chan')
- grad_skip: float32 [2048], P('chan')
The draws below stay inside these ranges and needn't reach their ends.
All inputs are finite; a program needn't handle non-finite values.
Results may differ from the reference program's by a relative error of at most 0.00011.
Values sent between devices are 32-bit elements; how exact they have to be, the bound alone decides.
A program may use at most 128 MiB of HBM per device.

```python
import math
import jax
import jax.numpy as jnp
from jax import lax

CH = 2048
KW = 7
TOKENS = 2048


def block_scale(key, shape, pieces, smallest, high):
    level, own = 1.0, jax.random.fold_in(key, 6)
    for dim, parts in pieces:
        heights = jnp.exp(jax.random.uniform(jax.random.fold_in(own, dim), (parts,), jnp.float32, smallest / len(pieces), high / len(pieces)))
        level = level * jnp.repeat(heights, shape[dim] // parts).reshape([-1 if axis == dim else 1 for axis in range(len(shape))])
    return level


def normal_values(own_key, shape, scale, most, cuts=(), dtype=jnp.bfloat16):
    entries = scale * jax.random.normal(own_key, shape, jnp.float32)
    if cuts:
        entries = entries * block_scale(own_key, shape, cuts, -0.22, 0.18)
    return jnp.clip(entries, -most, most).astype(dtype)


def setup_inputs(seed: int = 0) -> dict:
    key_list = jax.random.split(jax.random.key(seed), 8)
    return {
        "signal": normal_values(key_list[0], (CH, TOKENS), 1.0, 6.0, ((0, 4), (1, 8)), jnp.float32),
        "gate_in": normal_values(key_list[1], (CH, TOKENS), 1.0, 6.0, ((0, 4), (1, 8)), jnp.float32),
        "filter_raw": normal_values(key_list[2], (CH, TOKENS), 1.0, 6.0, ((0, 4), (1, 8)), jnp.float32),
        "short_kernel": normal_values(key_list[3], (CH, KW), KW ** -0.5, 2.0, ((0, 4),), jnp.float32),
        "skip_gain": normal_values(key_list[4], (CH,), 1.0, 4.0, ((0, 4),), jnp.float32),
        "out_weight": normal_values(key_list[5], (CH, CH), CH ** -0.5, 0.125, ((1, 4),), jnp.float32),
        "cotangent": normal_values(key_list[6], (CH, TOKENS), 1.0, 6.0, ((0, 4), (1, 8)), jnp.float32),
    }


def causal_taps(series, short_kernel):
    kernel_taps = short_kernel.shape[1]
    length = series.shape[1]
    padded = jnp.pad(series, ((0, 0), (kernel_taps - 1, 0)))
    result = jnp.zeros_like(series)
    for j in range(kernel_taps):
        result = result + short_kernel[:, j:j + 1] * padded[:, kernel_taps - 1 - j:kernel_taps - 1 - j + length]
    return (result, padded)

def channel_block(operands):
    signal, gate_in, filter_raw, short_kernel, skip_gain, grad_mix = operands
    scale_factor = 1.0 / math.sqrt(TOKENS)
    kernel_taps = short_kernel.shape[1]
    length = signal.shape[1]
    doubled = 2 * length
    conv_in, padded = causal_taps(signal, short_kernel)
    long_filter = filter_raw * scale_factor
    filter_spec = jnp.fft.rfft(long_filter, n=doubled, axis=1)
    value_spec = jnp.fft.rfft(conv_in, n=doubled, axis=1)
    long_conv = jnp.fft.irfft(filter_spec * value_spec, n=doubled, axis=1)[:, :length]
    response = long_conv + skip_gain[:, None] * conv_in
    grad_gate = grad_mix * response
    grad_resp = grad_mix * gate_in
    grad_spec = jnp.fft.rfft(grad_resp, n=doubled, axis=1)
    grad_value = jnp.fft.irfft(jnp.conj(filter_spec) * grad_spec, n=doubled, axis=1)[:, :length]
    grad_value = grad_value + skip_gain[:, None] * grad_resp
    grad_filter = jnp.fft.irfft(jnp.conj(value_spec) * grad_spec, n=doubled, axis=1)[:, :length] * scale_factor
    extended = jnp.pad(grad_value, ((0, 0), (0, kernel_taps - 1)))
    grad_signal = jnp.zeros_like(grad_value)
    for j in range(kernel_taps):
        grad_signal = grad_signal + short_kernel[:, j:j + 1] * extended[:, j:j + length]
    grad_kernel = jnp.stack([lax.optimization_barrier(jnp.sum(grad_value * padded[:, kernel_taps - 1 - j:kernel_taps - 1 - j + length], axis=1)) for j in range(kernel_taps)], axis=1) * scale_factor
    grad_skip = lax.optimization_barrier(jnp.sum(grad_resp * conv_in, axis=1)) * scale_factor
    return (grad_gate, grad_signal, grad_filter, grad_kernel, grad_skip)

def reference(signal, gate_in, filter_raw, short_kernel, skip_gain, out_weight, cotangent):
    grad_mix = jnp.dot(out_weight.T, cotangent, precision=lax.Precision.HIGHEST, preferred_element_type=jnp.float32)
    block_size = 16 if CH % 16 == 0 else CH
    groups = CH // block_size

    def split_rows(array):
        return array.reshape((groups, block_size) + array.shape[1:])
    results = lax.map(channel_block, tuple((split_rows(array) for array in (signal, gate_in, filter_raw, short_kernel, skip_gain, grad_mix))))
    grad_gate, grad_signal, grad_filter, grad_kernel, grad_skip = results
    return (grad_gate.reshape(CH, TOKENS), grad_signal.reshape(CH, TOKENS), grad_filter.reshape(CH, TOKENS), grad_kernel.reshape(CH, KW), grad_skip.reshape(CH))
```

```python
import functools
import math

import jax
import jax.numpy as jnp
import numpy as np
from jax import lax
from jax.experimental import pallas as pl
from jax.experimental.pallas import tpu as pltpu
from jax.sharding import PartitionSpec as P

MESH = pl.DeviceIdType.MESH
F32 = jnp.float32
BF16 = jnp.bfloat16
SIG, FIL, RESP, GSIG, GFIL, SMALL, GRAD = range(7)


def split_bf16(value):
    high = value.astype(BF16)
    return high, (value - high.astype(F32)).astype(BF16)


def tables(blocks, length, scale):
    total = 2 * blocks * length
    turn = np.arange(blocks + 1)[:, None] * np.arange(length)[None, :] % total
    angle = 2.0 * np.pi / total * turn
    weight = np.full((blocks + 1, 1), 2.0)
    weight[0] = weight[blocks] = 1.0
    weight = weight * (scale / total)
    twiddle = np.stack(
        (np.cos(angle), np.sin(angle), weight * np.cos(angle), weight * np.sin(angle))
    ).astype(np.float32)
    turn = np.arange(length)[:, None] * np.arange(length)[None, :] % length
    angle = 2.0 * np.pi / length * turn
    cosine, sine = np.cos(angle), np.sin(angle)
    matrix = np.block([[cosine, -sine], [sine, cosine]]).astype(np.float32)
    high = matrix.astype(jnp.bfloat16)
    low = (matrix - high.astype(np.float32)).astype(jnp.bfloat16)
    return twiddle, high, low


def weighted_sum(terms):
    total = None
    for factor, value in terms:
        if abs(factor) < 1e-12:
            continue
        if abs(factor - 1.0) < 1e-12:
            part = value
        elif abs(factor + 1.0) < 1e-12:
            part = -value
        else:
            part = np.float32(factor) * value
        total = part if total is None else total + part
    return total


def forward_blocks(parts, twiddle, store):
    blocks = len(parts)

    def put(q, real, imag):
        cosine, sine = twiddle[0, q : q + 1, :], twiddle[1, q : q + 1, :]
        if imag is None:
            store(q, real * cosine, -real * sine)
        else:
            store(q, real * cosine + imag * sine, imag * cosine - real * sine)

    for q in range(blocks // 2 + 1):
        def gather(first, trig, sign):
            return weighted_sum(
                [(sign * trig(math.pi * a * q / blocks), parts[a]) for a in range(first, blocks, 2)]
            )

        even_re, even_im = gather(0, math.cos, 1.0), gather(0, math.sin, -1.0)
        odd_re, odd_im = gather(1, math.cos, 1.0), gather(1, math.sin, -1.0)

        def add(a, b, sign_a, sign_b):
            return weighted_sum([(s, v) for s, v in ((sign_a, a), (sign_b, b)) if v is not None])

        put(q, add(even_re, odd_re, 1.0, 1.0), add(even_im, odd_im, 1.0, 1.0))
        if q != blocks - q:
            put(blocks - q, add(even_re, odd_re, 1.0, -1.0), add(even_im, odd_im, -1.0, 1.0))


def inverse_blocks(blocks, length, twiddle, load):
    def real_imag(q):
        pair = load(q)
        real, minus = pair[:, :length], pair[:, length:]
        cosine, sine = twiddle[2, q : q + 1, :], twiddle[3, q : q + 1, :]
        return real * cosine + minus * sine, real * sine - minus * cosine

    first, last = real_imag(0)[0], real_imag(blocks)[0]
    half_re, half_im = real_imag(blocks // 2)
    pairs = []
    for q in range(1, blocks // 2):
        (re_a, im_a), (re_b, im_b) = real_imag(q), real_imag(blocks - q)
        pairs.append((re_a + re_b, im_a - im_b, re_a - re_b, im_a + im_b))
    result = []
    for a in range(blocks):
        odd = a % 2
        terms = [(1.0, first - last if odd else first + last)]
        terms.append((math.cos(math.pi * a / 2), half_re))
        terms.append((-math.sin(math.pi * a / 2), half_im))
        for q in range(1, blocks // 2):
            angle = math.pi * a * q / blocks
            terms.append((math.cos(angle), pairs[q - 1][2 * odd]))
            terms.append((-math.sin(angle), pairs[q - 1][2 * odd + 1]))
        result.append(weighted_sum(terms))
    return result


def kernel(
    dims,
    sig_in, gate_in, fil_in, taps_ref, w_in, cot_in, twiddle, high_ref, low_ref,
    gate_out, gsig_out, gfil_out, small_out,
    w_buf, wt_hi, wt_lo, cot_all, mix, gate_buf, sig_buf, fil_buf, conv_buf,
    resp_send, resp_buf, grad_send, grad_buf, gsig_send, gfil_send, small_buf, small_send,
    stage, fil_spec, val_spec, grad_spec, work,
    up_sem, down_sem, line_sem, send_sem, recv_sem, local_sem, load_sem,
):
    devices, groups, rows, rows_pad, length, taps, halves, scale = dims
    me, chan = lax.axis_index("ctx"), lax.axis_index("chan")
    half_len = length // halves
    group_rows = min(8, rows)
    row_steps = rows // group_rows
    classes = devices + 1
    chunk = 3 if classes % 3 == 0 else 1

    w_copy = pltpu.make_async_copy(w_in, w_buf, load_sem.at[0])
    gate_copy = pltpu.make_async_copy(gate_in, gate_buf, load_sem.at[1])
    cot_copy = pltpu.make_async_copy(cot_in, cot_all.at[chan], load_sem.at[2])
    w_copy.start()
    cot_copy.start()
    gate_copy.start()

    barrier = pltpu.get_barrier_semaphore()

    @pl.loop(1, devices)
    def _(k):
        pl.semaphore_signal(
            barrier, inc=1, device_id={"ctx": lax.rem(me + k, devices)}, device_id_type=MESH
        )

    @pl.loop(1, groups)
    def _(k):
        pl.semaphore_signal(
            barrier, inc=1, device_id={"chan": lax.rem(chan + k, groups)}, device_id_type=MESH
        )

    pl.semaphore_wait(barrier, devices + groups - 2)

    def lanes(h):
        return pl.ds(h * half_len, half_len)

    def hop(step, h, up):
        block = chan - step if up else chan + step
        source = cot_in if step == 0 else cot_all.at[block]
        sems = up_sem if up else down_sem
        return pltpu.make_async_remote_copy(
            src_ref=source.at[:, lanes(h)],
            dst_ref=cot_all.at[block, :, lanes(h)],
            send_sem=sems.at[h, step],
            recv_sem=line_sem.at[h, block],
            device_id={"chan": chan + 1 if up else chan - 1},
            device_id_type=MESH,
        )

    def sends(step, up):
        if up:
            return jnp.logical_and(chan - step >= 0, chan + 1 < groups)
        return jnp.logical_and(chan + step < groups, chan >= 1)

    def arrives(step, up):
        return chan - step >= 0 if up else chan + step < groups

    def line_start(step, h):
        for up in (True, False):
            @pl.when(sends(step, up))
            def _():
                hop(step, h, up).start()

    def line_arrive(step, h):
        for up in (True, False):
            @pl.when(arrives(step, up))
            def _():
                block = chan - step if up else chan + step
                slot = cot_all.at[block, :, lanes(h)]
                pltpu.make_async_remote_copy(
                    src_ref=slot,
                    dst_ref=slot,
                    send_sem=up_sem.at[h, step],
                    recv_sem=line_sem.at[h, block],
                    device_id={"chan": chan - 1 if up else chan + 1},
                    device_id_type=MESH,
                ).wait_recv()

                @pl.when(sends(step, up))
                def _():
                    hop(step, h, up).start()

    def all_to_all(index, source, target):
        def piece(k):
            peer = lax.rem(me + k, devices)
            return pltpu.make_async_remote_copy(
                src_ref=source(peer),
                dst_ref=target(me),
                send_sem=send_sem.at[index, k],
                recv_sem=recv_sem.at[index, k],
                device_id={"ctx": peer},
                device_id_type=MESH,
            )

        own = pltpu.make_async_copy(source(me), target(me), local_sem.at[index])

        def start():
            @pl.loop(1, devices)
            def _(k):
                piece(k).start()

            own.start()

        def arrive():
            @pl.loop(1, devices)
            def _(k):
                piece(k).wait_recv()

            own.wait()

        def sent():
            @pl.loop(1, devices)
            def _(k):
                piece(k).wait_send()

        return start, arrive, sent

    sig_start, sig_arrive, sig_sent = all_to_all(SIG, lambda p: sig_in.at[p], lambda p: sig_buf.at[p])
    fil_start, fil_arrive, fil_sent = all_to_all(FIL, lambda p: fil_in.at[p], lambda p: fil_buf.at[p])
    resp_start, resp_arrive, resp_sent = all_to_all(
        RESP, lambda p: resp_send.at[p], lambda p: resp_buf.at[p]
    )
    gsig_start, gsig_arrive, gsig_sent = all_to_all(
        GSIG, lambda p: gsig_send.at[p], lambda p: gsig_out.at[p]
    )
    gfil_start, gfil_arrive, gfil_sent = all_to_all(
        GFIL, lambda p: gfil_send.at[p], lambda p: gfil_out.at[p]
    )
    small_start, small_arrive, small_sent = all_to_all(
        SMALL, lambda p: small_send, lambda p: small_out.at[p]
    )
    grad_moves = [
        all_to_all(
            GRAD + h,
            lambda p, h=h: grad_send.at[p, :, lanes(h)],
            lambda p, h=h: grad_buf.at[p, :, lanes(h)],
        )
        for h in range(halves)
    ]

    for h in range(halves):
        line_start(0, h)
    sig_start()
    fil_start()

    def dft(read, target):
        @pl.loop(0, classes // chunk)
        def _(i):
            at = pl.ds(i * chunk, chunk)
            high, low = split_bf16(read(at))
            result = jnp.dot(high, low_ref[...], preferred_element_type=F32)
            result = result + jnp.dot(low, high_ref[...], preferred_element_type=F32)
            result = result + jnp.dot(high, high_ref[...], preferred_element_type=F32)
            target[at] = result.reshape(chunk, rows_pad, 2 * length)

    def plain(at):
        return stage[at].reshape(chunk * rows_pad, 2 * length)

    def product(first, second, conjugate):
        def read(at):
            a_re, a_im = first[at, :, :length], first[at, :, length:]
            b_re, b_im = second[at, :, :length], second[at, :, length:]
            if conjugate:
                real, minus = a_re * b_re + a_im * b_im, a_im * b_re - a_re * b_im
            else:
                real, minus = a_re * b_re - a_im * b_im, -(a_re * b_im + a_im * b_re)
            return jnp.concatenate((real, minus), axis=2).reshape(chunk * rows_pad, 2 * length)

        return read

    def over_rows(body):
        @pl.loop(0, row_steps)
        def _(r):
            body(pl.ds(pl.multiple_of(r * group_rows, group_rows), group_rows))

    def stage_store(at):
        def store(q, real, imag):
            stage[q, at, :length] = real
            stage[q, at, length:] = imag

        return store

    def tap_rows(at):
        return taps_ref[me, at, :]

    def delayed(parts, a, j):
        if j == 0:
            return parts[a]
        before = jnp.zeros_like(parts[a][:, :128]) if a == 0 else parts[a - 1][:, length - 128 :]
        joined = jnp.concatenate((before, parts[a]), axis=1)
        return pltpu.roll(joined, j, 1)[:, 128:]

    def advanced(parts, a, j):
        if j == 0:
            return parts[a]
        after = jnp.zeros_like(parts[a][:, :128]) if a == devices - 1 else parts[a + 1][:, :128]
        joined = jnp.concatenate((parts[a], after), axis=1)
        return pltpu.roll(joined, length + 128 - j, 1)[:, :length]

    w_copy.wait()

    @pl.loop(0, groups)
    def _(g):
        turned = w_buf[g].T
        high, low = split_bf16(turned)
        wt_hi[g] = high
        wt_lo[g] = low

    cot_copy.wait()

    def mix_add(block, h, first):
        high, low = split_bf16(cot_all[block, :, h * half_len : (h + 1) * half_len])
        result = jnp.dot(wt_lo[block], high, preferred_element_type=F32)
        result = result + jnp.dot(wt_hi[block], low, preferred_element_type=F32)
        result = result + jnp.dot(wt_hi[block], high, preferred_element_type=F32)
        at = (slice(None), slice(h * half_len, (h + 1) * half_len))
        mix[at] = result if first else mix[at] + result

    def mix_step(step, h):
        for up in (True, False):
            @pl.when(arrives(step, up))
            def _():
                mix_add(chan - step if up else chan + step, h, False)

    for h in range(halves):
        mix_add(chan, h, True)

    sig_arrive()

    def conv_rows(at):
        tap = tap_rows(at)
        parts = [sig_buf[a, at, :] for a in range(devices)]
        conv = []
        for a in range(devices):
            total = tap[:, :1] * parts[a]
            for j in range(1, taps):
                total = total + tap[:, j : j + 1] * delayed(parts, a, j)
            conv_buf[a, at, :] = total
            conv.append(total)
        forward_blocks(conv, twiddle, stage_store(at))

    over_rows(conv_rows)
    dft(plain, val_spec)

    for h in range(halves):
        if groups > 1:
            line_arrive(1, h)

    fil_arrive()
    over_rows(
        lambda at: forward_blocks(
            [fil_buf[a, at, :] for a in range(devices)], twiddle, stage_store(at)
        )
    )
    dft(plain, fil_spec)
    if groups > 1:
        for h in range(halves):
            mix_step(1, h)
    dft(product(fil_spec, val_spec, False), work)

    def resp_rows(at):
        skip = tap_rows(at)[:, taps : taps + 1]
        conv = inverse_blocks(devices, length, twiddle, lambda q: work[q, at, :])
        for a in range(devices):
            resp_send[a, at, :] = conv[a] + skip * conv_buf[a, at, :]

    over_rows(resp_rows)
    resp_start()

    for step in range(2, groups - 1):
        for h in range(halves):
            line_arrive(step, h)
            mix_step(step, h)
    gate_copy.wait()
    for h in range(halves):
        if groups > 2:
            line_arrive(groups - 1, h)
            mix_step(groups - 1, h)
        here = slice(h * half_len, (h + 1) * half_len)
        for d in range(devices):
            grad_send[d, :, here] = mix[d * rows : (d + 1) * rows, here] * gate_buf[d, :, here]
        grad_moves[h][0]()

    resp_arrive()
    for d in range(devices):
        gate_out[d] = mix[d * rows : (d + 1) * rows, :] * resp_buf[d]

    for _, grad_arrive, _ in grad_moves:
        grad_arrive()

    over_rows(
        lambda at: forward_blocks(
            [grad_buf[a, at, :] for a in range(devices)], twiddle, stage_store(at)
        )
    )
    dft(plain, grad_spec)
    dft(product(val_spec, grad_spec, True), work)

    def filter_rows(at):
        parts = inverse_blocks(devices, length, twiddle, lambda q: work[q, at, :])
        for a in range(devices):
            gfil_send[a, at, :] = parts[a]

    over_rows(filter_rows)
    gfil_start()
    dft(product(fil_spec, grad_spec, True), work)

    def value_rows(at):
        tap = tap_rows(at)
        skip = tap[:, taps : taps + 1]
        value = inverse_blocks(devices, length, twiddle, lambda q: work[q, at, :])
        grad = [grad_buf[a, at, :] for a in range(devices)]
        value = [value[a] + skip * grad[a] for a in range(devices)]
        for a in range(devices):
            total = tap[:, :1] * value[a]
            for j in range(1, taps):
                total = total + tap[:, j : j + 1] * advanced(value, a, j)
            gsig_send[a, at, :] = total
        signal = [sig_buf[a, at, :] for a in range(devices)]
        lane = lax.broadcasted_iota(jnp.int32, (group_rows, 128), 1)
        sums = jnp.zeros((group_rows, 128), F32)
        for j in range(taps + 1):
            total = None
            for a in range(devices):
                if j < taps:
                    part = value[a] * delayed(signal, a, j)
                else:
                    part = grad[a] * conv_buf[a, at, :]
                total = part if total is None else total + part
            total = jnp.sum(total, axis=1, keepdims=True) * np.float32(scale)
            sums = jnp.where(lane == j, total, sums)
        small_buf[at, :] = sums

    small_buf[...] = jnp.zeros_like(small_buf)
    over_rows(value_rows)
    gsig_start()
    small_send[...] = small_buf[...].T[:8, :]
    small_start()

    for step in range(groups):
        for up in (True, False):
            @pl.when(sends(step, up))
            def _():
                for h in range(halves):
                    hop(step, h, up).wait_send()

    sig_sent()
    fil_sent()
    resp_sent()
    for _, _, grad_sent in grad_moves:
        grad_sent()
    gfil_sent()
    gsig_sent()
    small_sent()
    gfil_arrive()
    gsig_arrive()
    small_arrive()


def per_device(signal, gate_in, filter_raw, short_kernel, skip_gain, out_weight, cotangent):
    channels, length = signal.shape
    taps = short_kernel.shape[1]
    devices, groups = lax.axis_size("ctx"), lax.axis_size("chan")
    rows = channels // devices
    rows_pad = max(rows, 8)
    halves = 2
    scale = 1.0 / math.sqrt(length * devices)
    twiddle, high, low = tables(devices, length, scale)
    shape = (devices, rows, length)
    tap_table = jnp.concatenate((short_kernel, skip_gain[:, None]), axis=1)
    tap_table = tap_table.reshape(devices, rows, taps + 1)
    out_rows = cotangent.shape[0]
    spec_shape = (devices + 1, rows_pad, 2 * length)
    dims = (devices, groups, rows, rows_pad, length, taps, halves, scale)
    moves = GRAD + halves

    def vmem(*size, dtype=F32):
        return pltpu.VMEM(size, dtype)

    in_vmem, anywhere = pl.BlockSpec(memory_space=pltpu.VMEM), pl.BlockSpec(memory_space=pl.ANY)
    block = jax.ShapeDtypeStruct(shape, F32)
    grad_gate, grad_signal, grad_filter, small = pl.pallas_call(
        functools.partial(kernel, dims),
        out_shape=(block, block, block, jax.ShapeDtypeStruct((devices, 8, 128), F32)),
        in_specs=[anywhere, anywhere, anywhere, in_vmem, anywhere, anywhere, in_vmem, in_vmem, in_vmem],
        out_specs=(in_vmem, anywhere, anywhere, anywhere),
        scratch_shapes=[
            vmem(groups, out_rows, channels),
            vmem(groups, channels, out_rows, dtype=BF16),
            vmem(groups, channels, out_rows, dtype=BF16),
            vmem(groups, out_rows, length),
            vmem(channels, length),
            *[vmem(*shape) for _ in range(10)],
            vmem(128, 128),
            vmem(8, 128),
            *[vmem(*spec_shape) for _ in range(5)],
            pltpu.SemaphoreType.DMA((halves, groups)),
            pltpu.SemaphoreType.DMA((halves, groups)),
            pltpu.SemaphoreType.DMA((halves, groups)),
            pltpu.SemaphoreType.DMA((moves, devices)),
            pltpu.SemaphoreType.DMA((moves, devices)),
            pltpu.SemaphoreType.DMA((moves,)),
            pltpu.SemaphoreType.DMA((3,)),
        ],
        compiler_params=pltpu.CompilerParams(
            collective_id=0, has_side_effects=True, vmem_limit_bytes=56 * 2**20
        ),
    )(
        signal.reshape(shape),
        gate_in.reshape(shape),
        filter_raw.reshape(shape),
        tap_table,
        out_weight.reshape(groups, out_rows, channels),
        cotangent,
        jnp.asarray(twiddle),
        jnp.asarray(high),
        jnp.asarray(low),
    )
    sums = jnp.transpose(small[:, : taps + 1, :rows], (0, 2, 1)).reshape(channels, taps + 1)
    whole = (channels, length)
    return (
        grad_gate.reshape(whole),
        grad_signal.reshape(whole),
        grad_filter.reshape(whole),
        sums[:, :taps],
        sums[:, taps],
    )


def solution(mesh):
    placed = (
        P("chan", "ctx"),
        P("chan", "ctx"),
        P("chan", "ctx"),
        P("chan", None),
        P("chan"),
        P(None, "chan"),
        P("chan", "ctx"),
    )
    return jax.shard_map(
        per_device,
        mesh=mesh,
        in_specs=placed,
        out_specs=(
            P("chan", "ctx"),
            P("chan", "ctx"),
            P("chan", "ctx"),
            P("chan", None),
            P("chan"),
        ),
        check_vma=False,
    )
```

```python
import functools
import math

import jax
import jax.numpy as jnp
import numpy as np
from jax import lax
from jax.experimental import pallas as pl
from jax.experimental.pallas import tpu as pltpu
from jax.sharding import PartitionSpec as P

MESH = pl.DeviceIdType.MESH
F32 = jnp.float32
BF16 = jnp.bfloat16
SIG, FIL, RESP, SMALL, MOVES = range(5)


def split_bf16(value):
    high = value.astype(BF16)
    return high, (value - high.astype(F32)).astype(BF16)


def tables(blocks, length, scale):
    total = 2 * blocks * length
    turn = np.arange(blocks + 1)[:, None] * np.arange(length)[None, :] % total
    angle = 2.0 * np.pi / total * turn
    weight = np.full((blocks + 1, 1), 2.0)
    weight[0] = weight[blocks] = 1.0
    weight = weight * (scale / total)
    twiddle = np.stack(
        (np.cos(angle), np.sin(angle), weight * np.cos(angle), weight * np.sin(angle))
    ).astype(np.float32)
    turn = np.arange(length)[:, None] * np.arange(length)[None, :] % length
    angle = 2.0 * np.pi / length * turn
    cosine, sine = np.cos(angle), np.sin(angle)
    matrix = np.block([[cosine, -sine], [sine, cosine]]).astype(np.float32)
    high = matrix.astype(jnp.bfloat16)
    low = (matrix - high.astype(np.float32)).astype(jnp.bfloat16)
    return twiddle, high, low


def weighted_sum(terms):
    total = None
    for factor, value in terms:
        if abs(factor) < 1e-12:
            continue
        if abs(factor - 1.0) < 1e-12:
            part = value
        elif abs(factor + 1.0) < 1e-12:
            part = -value
        else:
            part = np.float32(factor) * value
        total = part if total is None else total + part
    return total


def forward_blocks(parts, twiddle, store):
    blocks = len(parts)

    def put(q, real, imag):
        cosine, sine = twiddle[0, q : q + 1, :], twiddle[1, q : q + 1, :]
        if imag is None:
            store(q, real * cosine, -real * sine)
        else:
            store(q, real * cosine + imag * sine, imag * cosine - real * sine)

    for q in range(blocks // 2 + 1):
        def gather(first, trig, sign):
            return weighted_sum(
                [(sign * trig(math.pi * a * q / blocks), parts[a]) for a in range(first, blocks, 2)]
            )

        even_re, even_im = gather(0, math.cos, 1.0), gather(0, math.sin, -1.0)
        odd_re, odd_im = gather(1, math.cos, 1.0), gather(1, math.sin, -1.0)

        def add(a, b, sign_a, sign_b):
            return weighted_sum([(s, v) for s, v in ((sign_a, a), (sign_b, b)) if v is not None])

        put(q, add(even_re, odd_re, 1.0, 1.0), add(even_im, odd_im, 1.0, 1.0))
        if q != blocks - q:
            put(blocks - q, add(even_re, odd_re, 1.0, -1.0), add(even_im, odd_im, -1.0, 1.0))


def inverse_blocks(blocks, length, twiddle, load):
    def real_imag(q):
        pair = load(q)
        real, minus = pair[:, :length], pair[:, length:]
        cosine, sine = twiddle[2, q : q + 1, :], twiddle[3, q : q + 1, :]
        return real * cosine + minus * sine, real * sine - minus * cosine

    first, last = real_imag(0)[0], real_imag(blocks)[0]
    half_re, half_im = real_imag(blocks // 2)
    pairs = []
    for q in range(1, blocks // 2):
        (re_a, im_a), (re_b, im_b) = real_imag(q), real_imag(blocks - q)
        pairs.append((re_a + re_b, im_a - im_b, re_a - re_b, im_a + im_b))
    result = []
    for a in range(blocks):
        odd = a % 2
        terms = [(1.0, first - last if odd else first + last)]
        terms.append((math.cos(math.pi * a / 2), half_re))
        terms.append((-math.sin(math.pi * a / 2), half_im))
        for q in range(1, blocks // 2):
            angle = math.pi * a * q / blocks
            terms.append((math.cos(angle), pairs[q - 1][2 * odd]))
            terms.append((-math.sin(angle), pairs[q - 1][2 * odd + 1]))
        result.append(weighted_sum(terms))
    return result


def kernel(
    dims,
    sig_in, gate_in, fil_in, taps_in, skip_in, w_in, cot_in, twiddle, high_ref, low_ref,
    gate_out, gsig_out, gfil_out, small_out,
    w_buf, wt_hi, wt_lo, cot_all, mix, gate_buf, sig_buf, fil_buf, conv_buf,
    resp_send, resp_buf, grad_send, grad_buf, gsig_send, gfil_send, taps_ref, small_buf, small_send, small_land,
    stage, fil_spec, val_spec, grad_spec, work,
    up_sem, down_sem, line_sem, send_sem, recv_sem, local_sem, load_sem,
):
    devices, groups, rows, length, taps, halves, parts_n, scale = dims
    me, chan = lax.axis_index("ctx"), lax.axis_index("chan")
    half_len = length // halves
    group_rows = min(8, rows)
    row_steps = rows // group_rows
    classes = devices + 1
    part_rows = rows // parts_n
    part_steps = row_steps // parts_n

    w_copy = pltpu.make_async_copy(w_in, w_buf, load_sem.at[0])
    gate_copy = pltpu.make_async_copy(gate_in, gate_buf, load_sem.at[1])
    cot_copy = pltpu.make_async_copy(cot_in, cot_all.at[chan], load_sem.at[2])
    w_copy.start()
    cot_copy.start()
    gate_copy.start()

    barrier = pltpu.get_barrier_semaphore()

    @pl.loop(1, devices)
    def _(k):
        pl.semaphore_signal(
            barrier, inc=1, device_id={"ctx": lax.rem(me + k, devices)}, device_id_type=MESH
        )

    @pl.loop(1, groups)
    def _(k):
        pl.semaphore_signal(
            barrier, inc=1, device_id={"chan": lax.rem(chan + k, groups)}, device_id_type=MESH
        )

    pl.semaphore_wait(barrier, devices + groups - 2)

    def lanes(h):
        return pl.ds(h * half_len, half_len)

    def hop(step, h, up):
        block = chan - step if up else chan + step
        source = cot_in if step == 0 else cot_all.at[block]
        sems = up_sem if up else down_sem
        return pltpu.make_async_remote_copy(
            src_ref=source.at[:, lanes(h)],
            dst_ref=cot_all.at[block, :, lanes(h)],
            send_sem=sems.at[h, step],
            recv_sem=line_sem.at[h, block],
            device_id={"chan": chan + 1 if up else chan - 1},
            device_id_type=MESH,
        )

    def sends(step, up):
        if up:
            return jnp.logical_and(chan - step >= 0, chan + 1 < groups)
        return jnp.logical_and(chan + step < groups, chan >= 1)

    def arrives(step, up):
        return chan - step >= 0 if up else chan + step < groups

    def line_start(step, h):
        for up in (True, False):
            @pl.when(sends(step, up))
            def _():
                hop(step, h, up).start()

    def line_arrive(step, h):
        for up in (True, False):
            @pl.when(arrives(step, up))
            def _():
                block = chan - step if up else chan + step
                slot = cot_all.at[block, :, lanes(h)]
                pltpu.make_async_remote_copy(
                    src_ref=slot,
                    dst_ref=slot,
                    send_sem=up_sem.at[h, step],
                    recv_sem=line_sem.at[h, block],
                    device_id={"chan": chan - 1 if up else chan + 1},
                    device_id_type=MESH,
                ).wait_recv()

                @pl.when(sends(step, up))
                def _():
                    hop(step, h, up).start()

    def all_to_all(index, source, target):
        def piece(k):
            peer = lax.rem(me + k, devices)
            return pltpu.make_async_remote_copy(
                src_ref=source(peer),
                dst_ref=target(me),
                send_sem=send_sem.at[index, k],
                recv_sem=recv_sem.at[index, k],
                device_id={"ctx": peer},
                device_id_type=MESH,
            )

        own = pltpu.make_async_copy(source(me), target(me), local_sem.at[index])

        def start():
            @pl.loop(1, devices)
            def _(k):
                piece(k).start()

            own.start()

        def arrive():
            @pl.loop(1, devices)
            def _(k):
                piece(k).wait_recv()

            own.wait()

        def sent():
            @pl.loop(1, devices)
            def _(k):
                piece(k).wait_send()

        return start, arrive, sent

    sig_start, sig_arrive, sig_sent = all_to_all(SIG, lambda p: sig_in.at[p], lambda p: sig_buf.at[p])
    fil_start, fil_arrive, fil_sent = all_to_all(FIL, lambda p: fil_in.at[p], lambda p: fil_buf.at[p])
    resp_start, resp_arrive, resp_sent = all_to_all(
        RESP, lambda p: resp_send.at[p], lambda p: resp_buf.at[p]
    )
    small_start, small_arrive, small_sent = all_to_all(
        SMALL, lambda p: small_send, lambda p: small_land.at[p]
    )

    def part_at(part):
        return pl.ds(part * part_rows, part_rows)

    grad_moves = [
        [
            all_to_all(
                MOVES + h * parts_n + part,
                lambda p, h=h, part=part: grad_send.at[p, part_at(part), lanes(h)],
                lambda p, h=h, part=part: grad_buf.at[p, part_at(part), lanes(h)],
            )
            for part in range(parts_n)
        ]
        for h in range(halves)
    ]
    back_moves = [
        [
            all_to_all(
                MOVES + (halves + which) * parts_n + part,
                lambda p, source=source, part=part: source.at[p, part_at(part)],
                lambda p, target=target, part=part: target.at[p, part_at(part)],
            )
            for part in range(parts_n)
        ]
        for which, (source, target) in enumerate(((gfil_send, gfil_out), (gsig_send, gsig_out)))
    ]

    for h in range(halves):
        line_start(0, h)
    sig_start()
    fil_start()

    def dft(read, target, part):
        span = max(part_rows, 8)
        at = (slice(None), slice(part * part_rows, part * part_rows + span))
        high, low = split_bf16(read(at).reshape(classes * span, 2 * length))
        result = jnp.dot(high, low_ref[...], preferred_element_type=F32)
        result = result + jnp.dot(low, high_ref[...], preferred_element_type=F32)
        result = result + jnp.dot(high, high_ref[...], preferred_element_type=F32)
        target[at] = result.reshape(classes, span, 2 * length)

    def plain(at):
        return stage[at]

    def product(first, second, conjugate):
        def read(at):
            a_re, a_im = first[at][:, :, :length], first[at][:, :, length:]
            b_re, b_im = second[at][:, :, :length], second[at][:, :, length:]
            if conjugate:
                real, minus = a_re * b_re + a_im * b_im, a_im * b_re - a_re * b_im
            else:
                real, minus = a_re * b_re - a_im * b_im, -(a_re * b_im + a_im * b_re)
            return jnp.concatenate((real, minus), axis=2)

        return read

    def over_rows(body, part):
        @pl.loop(part * part_steps, (part + 1) * part_steps)
        def _(r):
            body(pl.ds(pl.multiple_of(r * group_rows, group_rows), group_rows))

    def stage_store(at):
        def store(q, real, imag):
            stage[q, at, :length] = real
            stage[q, at, length:] = imag

        return store

    def tap_rows(at):
        return taps_ref[me, at, :]

    def delayed(parts, a, j):
        if j == 0:
            return parts[a]
        before = jnp.zeros_like(parts[a][:, :128]) if a == 0 else parts[a - 1][:, length - 128 :]
        joined = jnp.concatenate((before, parts[a]), axis=1)
        return pltpu.roll(joined, j, 1)[:, 128:]

    def advanced(parts, a, j):
        if j == 0:
            return parts[a]
        after = jnp.zeros_like(parts[a][:, :128]) if a == devices - 1 else parts[a + 1][:, :128]
        joined = jnp.concatenate((parts[a], after), axis=1)
        return pltpu.roll(joined, length + 128 - j, 1)[:, :length]

    w_copy.wait()

    @pl.loop(0, groups)
    def _(g):
        turned = w_buf[g].T
        high, low = split_bf16(turned)
        wt_hi[g] = high
        wt_lo[g] = low

    cot_copy.wait()

    channels = devices * rows
    table = jnp.concatenate(
        (taps_in[...], skip_in[...], jnp.zeros((128 - taps - 1, channels), F32)), axis=0
    )
    table = table.T
    for d in range(devices):
        taps_ref[d] = table[d * rows : (d + 1) * rows, :]

    def mix_add(block, h, first):
        high, low = split_bf16(cot_all[block, :, h * half_len : (h + 1) * half_len])
        result = jnp.dot(wt_lo[block], high, preferred_element_type=F32)
        result = result + jnp.dot(wt_hi[block], low, preferred_element_type=F32)
        result = result + jnp.dot(wt_hi[block], high, preferred_element_type=F32)
        at = (slice(None), slice(h * half_len, (h + 1) * half_len))
        mix[at] = result if first else mix[at] + result

    def mix_step(step, h):
        for up in (True, False):
            @pl.when(arrives(step, up))
            def _():
                mix_add(chan - step if up else chan + step, h, False)

    for h in range(halves):
        mix_add(chan, h, True)

    sig_arrive()

    def conv_rows(at):
        tap = tap_rows(at)
        parts = [sig_buf[a, at, :] for a in range(devices)]
        conv = []
        for a in range(devices):
            total = tap[:, :1] * parts[a]
            for j in range(1, taps):
                total = total + tap[:, j : j + 1] * delayed(parts, a, j)
            conv_buf[a, at, :] = total
            conv.append(total)
        forward_blocks(conv, twiddle, stage_store(at))

    for part in range(parts_n):
        over_rows(conv_rows, part)
        dft(plain, val_spec, part)

    for h in range(halves):
        if groups > 1:
            line_arrive(1, h)

    fil_arrive()
    for part in range(parts_n):
        over_rows(
            lambda at: forward_blocks(
                [fil_buf[a, at, :] for a in range(devices)], twiddle, stage_store(at)
            ),
            part,
        )
        dft(plain, fil_spec, part)
    if groups > 1:
        for h in range(halves):
            mix_step(1, h)

    def resp_rows(at):
        skip = tap_rows(at)[:, taps : taps + 1]
        conv = inverse_blocks(devices, length, twiddle, lambda q: work[q, at, :])
        for a in range(devices):
            resp_send[a, at, :] = conv[a] + skip * conv_buf[a, at, :]

    for part in range(parts_n):
        dft(product(fil_spec, val_spec, False), work, part)
        over_rows(resp_rows, part)
    resp_start()

    for step in range(2, groups - 1):
        for h in range(halves):
            line_arrive(step, h)
            mix_step(step, h)
    gate_copy.wait()
    for h in range(halves):
        if groups > 2:
            line_arrive(groups - 1, h)
            mix_step(groups - 1, h)
        here = slice(h * half_len, (h + 1) * half_len)
        for d in range(devices):
            grad_send[d, :, here] = mix[d * rows : (d + 1) * rows, here] * gate_buf[d, :, here]
        for part in range(parts_n):
            grad_moves[h][part][0]()

    resp_arrive()
    for d in range(devices):
        gate_out[d] = mix[d * rows : (d + 1) * rows, :] * resp_buf[d]

    def filter_rows(at):
        parts = inverse_blocks(devices, length, twiddle, lambda q: work[q, at, :])
        for a in range(devices):
            gfil_send[a, at, :] = parts[a]

    def value_rows(at):
        tap = tap_rows(at)
        skip = tap[:, taps : taps + 1]
        value = inverse_blocks(devices, length, twiddle, lambda q: work[q, at, :])
        grad = [grad_buf[a, at, :] for a in range(devices)]
        value = [value[a] + skip * grad[a] for a in range(devices)]
        sums = [None] * taps
        for a in range(devices):
            signal = sig_buf[a, at, :]
            total = None
            for j in range(taps):
                ahead = advanced(value, a, j)
                term, part_sum = tap[:, j : j + 1] * ahead, ahead * signal
                total = term if total is None else total + term
                sums[j] = part_sum if sums[j] is None else sums[j] + part_sum
            gsig_send[a, at, :] = total
        skip_sum = grad[0] * conv_buf[0, at, :]
        for a in range(1, devices):
            skip_sum = skip_sum + grad[a] * conv_buf[a, at, :]
        lane = lax.broadcasted_iota(jnp.int32, (group_rows, 128), 1)
        placed = jnp.zeros((group_rows, 128), F32)
        for j, each in enumerate(sums + [skip_sum]):
            total = jnp.sum(each, axis=1, keepdims=True) * np.float32(scale)
            placed = jnp.where(lane == j, total, placed)
        small_buf[at, :] = placed

    small_buf[...] = jnp.zeros_like(small_buf)
    for part in range(parts_n):
        for h in range(halves):
            grad_moves[h][part][1]()
        over_rows(
            lambda at: forward_blocks(
                [grad_buf[a, at, :] for a in range(devices)], twiddle, stage_store(at)
            ),
            part,
        )
        dft(plain, grad_spec, part)
        dft(product(val_spec, grad_spec, True), work, part)
        over_rows(filter_rows, part)
        back_moves[0][part][0]()
        dft(product(fil_spec, grad_spec, True), work, part)
        over_rows(value_rows, part)
        back_moves[1][part][0]()
    small_send[...] = small_buf[...].T[:8, :]
    small_start()

    for step in range(groups):
        for up in (True, False):
            @pl.when(sends(step, up))
            def _():
                for h in range(halves):
                    hop(step, h, up).wait_send()

    sig_sent()
    fil_sent()
    resp_sent()
    for move in grad_moves + back_moves:
        for part in range(parts_n):
            move[part][2]()
    small_sent()
    small_arrive()
    per_tile = 128 // rows
    for tile in range(-(-channels // 128)):
        total = None
        for i in range(min(per_tile, devices - tile * per_tile)):
            each = small_land[tile * per_tile + i]
            each = each if i == 0 else pltpu.roll(each, i * rows, 1)
            total = each if total is None else total + each
        width = min(128, channels - tile * 128)
        small_out[:, tile * 128 : tile * 128 + width] = total[:, :width]
    for move in back_moves:
        for part in range(parts_n):
            move[part][1]()


def handed_on(small_in, *refs):
    count = (len(refs) - 4) // 2
    arrays, results = refs[:count], refs[count : 2 * count]
    taps_out, skip_out, held, sems = refs[2 * count :]
    loads = [
        pltpu.make_async_copy(arrays[i], held.at[i], sems.at[0, i]) for i in range(count)
    ]
    stores = [
        pltpu.make_async_copy(held.at[i], results[i], sems.at[1, i]) for i in range(count)
    ]
    for load in loads:
        load.start()
    taps = taps_out.shape[0]
    taps_out[...] = small_in[:taps, :]
    skip_out[...] = small_in[taps : taps + 1, :]
    for load, store in zip(loads, stores):
        load.wait()
        store.start()
    for store in stores:
        store.wait()


def per_device(signal, gate_in, filter_raw, short_kernel, skip_gain, out_weight, cotangent):
    channels, length = signal.shape
    taps = short_kernel.shape[1]
    devices, groups = lax.axis_size("ctx"), lax.axis_size("chan")
    rows = channels // devices
    rows_pad = max(rows, 8)
    halves = 2
    scale = 1.0 / math.sqrt(length * devices)
    twiddle, high, low = tables(devices, length, scale)
    shape = (devices, rows, length)
    out_rows = cotangent.shape[0]
    parts_n = 2 if rows % 16 == 0 else 1
    spec_shape = (devices + 1, rows_pad, 2 * length)
    dims = (devices, groups, rows, length, taps, halves, parts_n, scale)
    moves = MOVES + (halves + 2) * parts_n

    def vmem(*size, dtype=F32):
        return pltpu.VMEM(size, dtype)

    in_vmem, anywhere = pl.BlockSpec(memory_space=pltpu.VMEM), pl.BlockSpec(memory_space=pl.ANY)
    block = jax.ShapeDtypeStruct(shape, F32)
    grad_gate, grad_signal, grad_filter, small = pl.pallas_call(
        functools.partial(kernel, dims),
        out_shape=(block, block, block, jax.ShapeDtypeStruct((8, channels), F32)),
        in_specs=[anywhere, anywhere, anywhere, in_vmem, in_vmem, anywhere, anywhere, in_vmem, in_vmem, in_vmem],
        out_specs=(in_vmem, anywhere, anywhere, in_vmem),
        scratch_shapes=[
            vmem(groups, out_rows, channels),
            vmem(groups, channels, out_rows, dtype=BF16),
            vmem(groups, channels, out_rows, dtype=BF16),
            vmem(groups, out_rows, length),
            vmem(channels, length),
            *[vmem(*shape) for _ in range(10)],
            vmem(devices, rows, 128),
            vmem(128, 128),
            vmem(8, 128),
            vmem(devices, 8, 128),
            *[vmem(*spec_shape) for _ in range(5)],
            pltpu.SemaphoreType.DMA((halves, groups)),
            pltpu.SemaphoreType.DMA((halves, groups)),
            pltpu.SemaphoreType.DMA((halves, groups)),
            pltpu.SemaphoreType.DMA((moves, devices)),
            pltpu.SemaphoreType.DMA((moves, devices)),
            pltpu.SemaphoreType.DMA((moves,)),
            pltpu.SemaphoreType.DMA((3,)),
        ],
        compiler_params=pltpu.CompilerParams(
            collective_id=0, has_side_effects=True, vmem_limit_bytes=56 * 2**20
        ),
    )(
        signal.reshape(shape),
        gate_in.reshape(shape),
        filter_raw.reshape(shape),
        short_kernel.T,
        skip_gain[None, :],
        out_weight.reshape(groups, out_rows, channels),
        cotangent,
        jnp.asarray(twiddle),
        jnp.asarray(high),
        jnp.asarray(low),
    )
    grad_gate, grad_signal, grad_filter, grad_kernel, grad_skip = pl.pallas_call(
        handed_on,
        out_shape=(block,) * 3
        + (
            jax.ShapeDtypeStruct((taps, channels), F32),
            jax.ShapeDtypeStruct((1, channels), F32),
        ),
        in_specs=[in_vmem] + [anywhere] * 3,
        out_specs=(anywhere,) * 3 + (in_vmem,) * 2,
        scratch_shapes=[vmem(3, *shape), pltpu.SemaphoreType.DMA((2, 3))],
    )(small, grad_gate, grad_signal, grad_filter)
    whole = (channels, length)
    return (
        grad_gate.reshape(whole),
        grad_signal.reshape(whole),
        grad_filter.reshape(whole),
        grad_kernel.T,
        grad_skip[0],
    )


def solution(mesh):
    placed = (
        P("chan", "ctx"),
        P("chan", "ctx"),
        P("chan", "ctx"),
        P("chan", None),
        P("chan"),
        P(None, "chan"),
        P("chan", "ctx"),
    )
    return jax.shard_map(
        per_device,
        mesh=mesh,
        in_specs=placed,
        out_specs=(
            P("chan", "ctx"),
            P("chan", "ctx"),
            P("chan", "ctx"),
            P("chan", None),
            P("chan"),
        ),
        check_vma=False,
    )
```

```python
import functools
import math

import jax
import jax.numpy as jnp
import numpy as np
from jax import lax
from jax.experimental import pallas as pl
from jax.experimental.pallas import tpu as pltpu
from jax.sharding import PartitionSpec as P

MESH = pl.DeviceIdType.MESH
F32 = jnp.float32
BF16 = jnp.bfloat16
SIG, FIL, RESP, SMALL, MOVES = range(5)


def split_bf16(value):
    high = value.astype(BF16)
    return high, (value - high.astype(F32)).astype(BF16)


def tables(blocks, length, scale):
    total = 2 * blocks * length
    turn = np.arange(blocks + 1)[:, None] * np.arange(length)[None, :] % total
    angle = 2.0 * np.pi / total * turn
    weight = np.full((blocks + 1, 1), 2.0)
    weight[0] = weight[blocks] = 1.0
    weight = weight * (scale / total)
    twiddle = np.stack(
        (np.cos(angle), np.sin(angle), weight * np.cos(angle), weight * np.sin(angle))
    ).astype(np.float32)
    turn = np.arange(length)[:, None] * np.arange(length)[None, :] % length
    angle = 2.0 * np.pi / length * turn
    cosine, sine = np.cos(angle), np.sin(angle)
    matrix = np.block([[cosine, -sine], [sine, cosine]]).astype(np.float32)
    high = matrix.astype(jnp.bfloat16)
    low = (matrix - high.astype(np.float32)).astype(jnp.bfloat16)
    return twiddle, high, low


def weighted_sum(terms):
    total = None
    for factor, value in terms:
        if abs(factor) < 1e-12:
            continue
        if abs(factor - 1.0) < 1e-12:
            part = value
        elif abs(factor + 1.0) < 1e-12:
            part = -value
        else:
            part = np.float32(factor) * value
        total = part if total is None else total + part
    return total


def forward_blocks(parts, twiddle, store):
    blocks = len(parts)

    def put(q, real, imag):
        cosine, sine = twiddle[0, q : q + 1, :], twiddle[1, q : q + 1, :]
        if imag is None:
            store(q, real * cosine, -real * sine)
        else:
            store(q, real * cosine + imag * sine, imag * cosine - real * sine)

    for q in range(blocks // 2 + 1):
        def gather(first, trig, sign):
            return weighted_sum(
                [(sign * trig(math.pi * a * q / blocks), parts[a]) for a in range(first, blocks, 2)]
            )

        even_re, even_im = gather(0, math.cos, 1.0), gather(0, math.sin, -1.0)
        odd_re, odd_im = gather(1, math.cos, 1.0), gather(1, math.sin, -1.0)

        def add(a, b, sign_a, sign_b):
            return weighted_sum([(s, v) for s, v in ((sign_a, a), (sign_b, b)) if v is not None])

        put(q, add(even_re, odd_re, 1.0, 1.0), add(even_im, odd_im, 1.0, 1.0))
        if q != blocks - q:
            put(blocks - q, add(even_re, odd_re, 1.0, -1.0), add(even_im, odd_im, -1.0, 1.0))


def inverse_blocks(blocks, length, twiddle, load):
    def real_imag(q):
        pair = load(q)
        real, minus = pair[:, :length], pair[:, length:]
        cosine, sine = twiddle[2, q : q + 1, :], twiddle[3, q : q + 1, :]
        return real * cosine + minus * sine, real * sine - minus * cosine

    first, last = real_imag(0)[0], real_imag(blocks)[0]
    half_re, half_im = real_imag(blocks // 2)
    pairs = []
    for q in range(1, blocks // 2):
        (re_a, im_a), (re_b, im_b) = real_imag(q), real_imag(blocks - q)
        pairs.append((re_a + re_b, im_a - im_b, re_a - re_b, im_a + im_b))
    result = []
    for a in range(blocks):
        odd = a % 2
        terms = [(1.0, first - last if odd else first + last)]
        terms.append((math.cos(math.pi * a / 2), half_re))
        terms.append((-math.sin(math.pi * a / 2), half_im))
        for q in range(1, blocks // 2):
            angle = math.pi * a * q / blocks
            terms.append((math.cos(angle), pairs[q - 1][2 * odd]))
            terms.append((-math.sin(angle), pairs[q - 1][2 * odd + 1]))
        result.append(weighted_sum(terms))
    return result


def kernel(
    dims,
    sig_in, gate_in, fil_in, taps_in, skip_in, w_in, cot_in, twiddle, high_ref, low_ref,
    gate_out, gsig_out, gfil_out, small_out,
    w_buf, wt_hi, wt_lo, cot_all, mix, gate_buf, sig_buf, fil_buf, conv_buf,
    resp_send, resp_buf, grad_send, grad_buf, gsig_send, gfil_send, taps_ref, small_buf, small_send, small_land,
    stage, fil_spec, val_spec, grad_spec, work,
    up_sem, down_sem, line_sem, send_sem, recv_sem, local_sem, load_sem,
):
    devices, groups, rows, length, taps, halves, parts_n, scale = dims
    me, chan = lax.axis_index("ctx"), lax.axis_index("chan")
    half_len = length // halves
    group_rows = min(8, rows)
    row_steps = rows // group_rows
    classes = devices + 1
    part_rows = rows // parts_n
    part_steps = row_steps // parts_n

    w_copy = pltpu.make_async_copy(w_in, w_buf, load_sem.at[0])
    gate_copy = pltpu.make_async_copy(gate_in, gate_buf, load_sem.at[1])
    cot_copy = pltpu.make_async_copy(cot_in, cot_all.at[chan], load_sem.at[2])
    w_copy.start()
    cot_copy.start()
    gate_copy.start()

    barrier = pltpu.get_barrier_semaphore()

    @pl.loop(1, devices)
    def _(k):
        pl.semaphore_signal(
            barrier, inc=1, device_id={"ctx": lax.rem(me + k, devices)}, device_id_type=MESH
        )

    @pl.loop(1, groups)
    def _(k):
        pl.semaphore_signal(
            barrier, inc=1, device_id={"chan": lax.rem(chan + k, groups)}, device_id_type=MESH
        )

    pl.semaphore_wait(barrier, devices + groups - 2)

    def lanes(h):
        return pl.ds(h * half_len, half_len)

    def hop(step, h, up):
        block = chan - step if up else chan + step
        source = cot_in if step == 0 else cot_all.at[block]
        sems = up_sem if up else down_sem
        return pltpu.make_async_remote_copy(
            src_ref=source.at[:, lanes(h)],
            dst_ref=cot_all.at[block, :, lanes(h)],
            send_sem=sems.at[h, step],
            recv_sem=line_sem.at[h, block],
            device_id={"chan": chan + 1 if up else chan - 1},
            device_id_type=MESH,
        )

    def sends(step, up):
        if up:
            return jnp.logical_and(chan - step >= 0, chan + 1 < groups)
        return jnp.logical_and(chan + step < groups, chan >= 1)

    def arrives(step, up):
        return chan - step >= 0 if up else chan + step < groups

    def line_start(step, h):
        for up in (True, False):
            @pl.when(sends(step, up))
            def _():
                hop(step, h, up).start()

    def line_arrive(step, h):
        for up in (True, False):
            @pl.when(arrives(step, up))
            def _():
                block = chan - step if up else chan + step
                slot = cot_all.at[block, :, lanes(h)]
                pltpu.make_async_remote_copy(
                    src_ref=slot,
                    dst_ref=slot,
                    send_sem=up_sem.at[h, step],
                    recv_sem=line_sem.at[h, block],
                    device_id={"chan": chan - 1 if up else chan + 1},
                    device_id_type=MESH,
                ).wait_recv()

                @pl.when(sends(step, up))
                def _():
                    hop(step, h, up).start()

    def all_to_all(index, source, target):
        def piece(k):
            peer = lax.rem(me + k, devices)
            return pltpu.make_async_remote_copy(
                src_ref=source(peer),
                dst_ref=target(me),
                send_sem=send_sem.at[index, k],
                recv_sem=recv_sem.at[index, k],
                device_id={"ctx": peer},
                device_id_type=MESH,
            )

        own = pltpu.make_async_copy(source(me), target(me), local_sem.at[index])

        def start():
            @pl.loop(1, devices)
            def _(k):
                piece(k).start()

            own.start()

        def arrive():
            @pl.loop(1, devices)
            def _(k):
                piece(k).wait_recv()

            own.wait()

        def sent():
            @pl.loop(1, devices)
            def _(k):
                piece(k).wait_send()

        return start, arrive, sent

    sig_start, sig_arrive, sig_sent = all_to_all(SIG, lambda p: sig_in.at[p], lambda p: sig_buf.at[p])
    fil_start, fil_arrive, fil_sent = all_to_all(FIL, lambda p: fil_in.at[p], lambda p: fil_buf.at[p])
    resp_start, resp_arrive, resp_sent = all_to_all(
        RESP, lambda p: resp_send.at[p], lambda p: resp_buf.at[p]
    )
    small_start, small_arrive, small_sent = all_to_all(
        SMALL, lambda p: small_send, lambda p: small_land.at[p]
    )

    def part_at(part):
        return pl.ds(part * part_rows, part_rows)

    grad_moves = [
        [
            all_to_all(
                MOVES + h * parts_n + part,
                lambda p, h=h, part=part: grad_send.at[p, part_at(part), lanes(h)],
                lambda p, h=h, part=part: grad_buf.at[p, part_at(part), lanes(h)],
            )
            for part in range(parts_n)
        ]
        for h in range(halves)
    ]
    back_moves = [
        [
            all_to_all(
                MOVES + (halves + which) * parts_n + part,
                lambda p, source=source, part=part: source.at[p, part_at(part)],
                lambda p, target=target, part=part: target.at[p, part_at(part)],
            )
            for part in range(parts_n)
        ]
        for which, (source, target) in enumerate(((gfil_send, gfil_out), (gsig_send, gsig_out)))
    ]

    for h in range(halves):
        line_start(0, h)
    sig_start()
    fil_start()

    def dft(read, target, part):
        span = max(part_rows, 8)
        at = (slice(None), slice(part * part_rows, part * part_rows + span))
        high, low = split_bf16(read(at).reshape(classes * span, 2 * length))
        result = jnp.dot(high, low_ref[...], preferred_element_type=F32)
        result = result + jnp.dot(low, high_ref[...], preferred_element_type=F32)
        result = result + jnp.dot(high, high_ref[...], preferred_element_type=F32)
        target[at] = result.reshape(classes, span, 2 * length)

    def plain(at):
        return stage[at]

    def product(first, second, conjugate):
        def read(at):
            a_re, a_im = first[at][:, :, :length], first[at][:, :, length:]
            b_re, b_im = second[at][:, :, :length], second[at][:, :, length:]
            if conjugate:
                real, minus = a_re * b_re + a_im * b_im, a_im * b_re - a_re * b_im
            else:
                real, minus = a_re * b_re - a_im * b_im, -(a_re * b_im + a_im * b_re)
            return jnp.concatenate((real, minus), axis=2)

        return read

    def over_rows(body, part):
        @pl.loop(part * part_steps, (part + 1) * part_steps)
        def _(r):
            body(pl.ds(pl.multiple_of(r * group_rows, group_rows), group_rows))

    def stage_store(at):
        def store(q, real, imag):
            stage[q, at, :length] = real
            stage[q, at, length:] = imag

        return store

    def tap_rows(at):
        return taps_ref[me, at, :]

    def delayed(parts, a, j):
        if j == 0:
            return parts[a]
        before = jnp.zeros_like(parts[a][:, :128]) if a == 0 else parts[a - 1][:, length - 128 :]
        joined = jnp.concatenate((before, parts[a]), axis=1)
        return pltpu.roll(joined, j, 1)[:, 128:]

    def advanced(parts, a, j):
        if j == 0:
            return parts[a]
        after = jnp.zeros_like(parts[a][:, :128]) if a == devices - 1 else parts[a + 1][:, :128]
        joined = jnp.concatenate((parts[a], after), axis=1)
        return pltpu.roll(joined, length + 128 - j, 1)[:, :length]

    w_copy.wait()

    @pl.loop(0, groups)
    def _(g):
        turned = w_buf[g].T
        high, low = split_bf16(turned)
        wt_hi[g] = high
        wt_lo[g] = low

    cot_copy.wait()

    channels = devices * rows
    table = jnp.concatenate(
        (taps_in[...], skip_in[...], jnp.zeros((128 - taps - 1, channels), F32)), axis=0
    )
    table = table.T
    for d in range(devices):
        taps_ref[d] = table[d * rows : (d + 1) * rows, :]

    def mix_add(block, h, first):
        high, low = split_bf16(cot_all[block, :, h * half_len : (h + 1) * half_len])
        result = jnp.dot(wt_lo[block], high, preferred_element_type=F32)
        result = result + jnp.dot(wt_hi[block], low, preferred_element_type=F32)
        result = result + jnp.dot(wt_hi[block], high, preferred_element_type=F32)
        at = (slice(None), slice(h * half_len, (h + 1) * half_len))
        mix[at] = result if first else mix[at] + result

    def mix_step(step, h):
        for up in (True, False):
            @pl.when(arrives(step, up))
            def _():
                mix_add(chan - step if up else chan + step, h, False)

    for h in range(halves):
        mix_add(chan, h, True)

    sig_arrive()

    def conv_rows(at):
        tap = tap_rows(at)
        parts = [sig_buf[a, at, :] for a in range(devices)]
        conv = []
        for a in range(devices):
            total = tap[:, :1] * parts[a]
            for j in range(1, taps):
                total = total + tap[:, j : j + 1] * delayed(parts, a, j)
            conv_buf[a, at, :] = total
            conv.append(total)
        forward_blocks(conv, twiddle, stage_store(at))

    for part in range(parts_n):
        over_rows(conv_rows, part)
        dft(plain, val_spec, part)

    for h in range(halves):
        if groups > 1:
            line_arrive(1, h)

    fil_arrive()
    for part in range(parts_n):
        over_rows(
            lambda at: forward_blocks(
                [fil_buf[a, at, :] for a in range(devices)], twiddle, stage_store(at)
            ),
            part,
        )
        dft(plain, fil_spec, part)
    if groups > 1:
        for h in range(halves):
            mix_step(1, h)

    def resp_rows(at):
        skip = tap_rows(at)[:, taps : taps + 1]
        conv = inverse_blocks(devices, length, twiddle, lambda q: work[q, at, :])
        for a in range(devices):
            resp_send[a, at, :] = conv[a] + skip * conv_buf[a, at, :]

    for part in range(parts_n):
        dft(product(fil_spec, val_spec, False), work, part)
        over_rows(resp_rows, part)
    resp_start()

    for step in range(2, groups - 1):
        for h in range(halves):
            line_arrive(step, h)
            mix_step(step, h)
    gate_copy.wait()
    for h in range(halves):
        if groups > 2:
            line_arrive(groups - 1, h)
            mix_step(groups - 1, h)
        here = slice(h * half_len, (h + 1) * half_len)
        for d in range(devices):
            grad_send[d, :, here] = mix[d * rows : (d + 1) * rows, here] * gate_buf[d, :, here]
        for part in range(parts_n):
            grad_moves[h][part][0]()

    resp_arrive()
    for d in range(devices):
        gate_out[d] = mix[d * rows : (d + 1) * rows, :] * resp_buf[d]

    def filter_rows(at):
        parts = inverse_blocks(devices, length, twiddle, lambda q: work[q, at, :])
        for a in range(devices):
            gfil_send[a, at, :] = parts[a]

    def value_rows(at):
        tap = tap_rows(at)
        skip = tap[:, taps : taps + 1]
        value = inverse_blocks(devices, length, twiddle, lambda q: work[q, at, :])
        grad = [grad_buf[a, at, :] for a in range(devices)]
        value = [value[a] + skip * grad[a] for a in range(devices)]
        sums = [None] * taps
        for a in range(devices):
            signal = sig_buf[a, at, :]
            total = None
            for j in range(taps):
                ahead = advanced(value, a, j)
                term, part_sum = tap[:, j : j + 1] * ahead, ahead * signal
                total = term if total is None else total + term
                sums[j] = part_sum if sums[j] is None else sums[j] + part_sum
            gsig_send[a, at, :] = total
        skip_sum = grad[0] * conv_buf[0, at, :]
        for a in range(1, devices):
            skip_sum = skip_sum + grad[a] * conv_buf[a, at, :]
        lane = lax.broadcasted_iota(jnp.int32, (group_rows, 128), 1)
        placed = jnp.zeros((group_rows, 128), F32)
        for j, each in enumerate(sums + [skip_sum]):
            total = jnp.sum(each, axis=1, keepdims=True) * np.float32(scale)
            placed = jnp.where(lane == j, total, placed)
        small_buf[at, :] = placed

    small_buf[...] = jnp.zeros_like(small_buf)
    for part in range(parts_n):
        for h in range(halves):
            grad_moves[h][part][1]()
        over_rows(
            lambda at: forward_blocks(
                [grad_buf[a, at, :] for a in range(devices)], twiddle, stage_store(at)
            ),
            part,
        )
        dft(plain, grad_spec, part)
        dft(product(val_spec, grad_spec, True), work, part)
        over_rows(filter_rows, part)
        back_moves[0][part][0]()
        dft(product(fil_spec, grad_spec, True), work, part)
        over_rows(value_rows, part)
        back_moves[1][part][0]()
    small_send[...] = small_buf[...].T[:8, :]
    small_start()

    for step in range(groups):
        for up in (True, False):
            @pl.when(sends(step, up))
            def _():
                for h in range(halves):
                    hop(step, h, up).wait_send()

    sig_sent()
    fil_sent()
    resp_sent()
    for move in grad_moves + back_moves:
        for part in range(parts_n):
            move[part][2]()
    small_sent()
    small_arrive()
    per_tile = 128 // rows
    for tile in range(-(-channels // 128)):
        total = None
        for i in range(min(per_tile, devices - tile * per_tile)):
            each = small_land[tile * per_tile + i]
            each = each if i == 0 else pltpu.roll(each, i * rows, 1)
            total = each if total is None else total + each
        width = min(128, channels - tile * 128)
        small_out[:, tile * 128 : tile * 128 + width] = total[:, :width]
    for move in back_moves:
        for part in range(parts_n):
            move[part][1]()


def handed_on(small_in, *refs):
    count = (len(refs) - 4) // 2
    arrays, results = refs[:count], refs[count : 2 * count]
    taps_out, skip_out, held, sems = refs[2 * count :]
    cuts = sems.shape[2]
    span = held.shape[1] // cuts
    pieces = [(i, k, pl.ds(k * span, span)) for k in range(cuts) for i in range(count)]
    loads = [
        pltpu.make_async_copy(arrays[i].at[at], held.at[i, at], sems.at[0, i, k])
        for i, k, at in pieces
    ]
    stores = [
        pltpu.make_async_copy(held.at[i, at], results[i].at[at], sems.at[1, i, k])
        for i, k, at in pieces
    ]
    for load in loads:
        load.start()
    taps = taps_out.shape[0]
    taps_out[...] = small_in[:taps, :]
    skip_out[...] = small_in[taps : taps + 1, :]
    for load, store in zip(loads, stores):
        load.wait()
        store.start()
    for store in stores:
        store.wait()


def per_device(signal, gate_in, filter_raw, short_kernel, skip_gain, out_weight, cotangent):
    channels, length = signal.shape
    taps = short_kernel.shape[1]
    devices, groups = lax.axis_size("ctx"), lax.axis_size("chan")
    rows = channels // devices
    rows_pad = max(rows, 8)
    halves = 2
    scale = 1.0 / math.sqrt(length * devices)
    twiddle, high, low = tables(devices, length, scale)
    shape = (devices, rows, length)
    out_rows = cotangent.shape[0]
    parts_n = 2 if rows % 16 == 0 else 1
    spec_shape = (devices + 1, rows_pad, 2 * length)
    dims = (devices, groups, rows, length, taps, halves, parts_n, scale)
    moves = MOVES + (halves + 2) * parts_n

    def vmem(*size, dtype=F32):
        return pltpu.VMEM(size, dtype)

    in_vmem, anywhere = pl.BlockSpec(memory_space=pltpu.VMEM), pl.BlockSpec(memory_space=pl.ANY)
    block = jax.ShapeDtypeStruct(shape, F32)
    grad_gate, grad_signal, grad_filter, small = pl.pallas_call(
        functools.partial(kernel, dims),
        out_shape=(block, block, block, jax.ShapeDtypeStruct((8, channels), F32)),
        in_specs=[anywhere, anywhere, anywhere, in_vmem, in_vmem, anywhere, anywhere, in_vmem, in_vmem, in_vmem],
        out_specs=(in_vmem, anywhere, anywhere, in_vmem),
        scratch_shapes=[
            vmem(groups, out_rows, channels),
            vmem(groups, channels, out_rows, dtype=BF16),
            vmem(groups, channels, out_rows, dtype=BF16),
            vmem(groups, out_rows, length),
            vmem(channels, length),
            *[vmem(*shape) for _ in range(10)],
            vmem(devices, rows, 128),
            vmem(128, 128),
            vmem(8, 128),
            vmem(devices, 8, 128),
            *[vmem(*spec_shape) for _ in range(5)],
            pltpu.SemaphoreType.DMA((halves, groups)),
            pltpu.SemaphoreType.DMA((halves, groups)),
            pltpu.SemaphoreType.DMA((halves, groups)),
            pltpu.SemaphoreType.DMA((moves, devices)),
            pltpu.SemaphoreType.DMA((moves, devices)),
            pltpu.SemaphoreType.DMA((moves,)),
            pltpu.SemaphoreType.DMA((3,)),
        ],
        compiler_params=pltpu.CompilerParams(
            collective_id=0, has_side_effects=True, vmem_limit_bytes=56 * 2**20
        ),
    )(
        signal.reshape(shape),
        gate_in.reshape(shape),
        filter_raw.reshape(shape),
        short_kernel.T,
        skip_gain[None, :],
        out_weight.reshape(groups, out_rows, channels),
        cotangent,
        jnp.asarray(twiddle),
        jnp.asarray(high),
        jnp.asarray(low),
    )
    grad_gate, grad_signal, grad_filter, grad_kernel, grad_skip = pl.pallas_call(
        handed_on,
        out_shape=(block,) * 3
        + (
            jax.ShapeDtypeStruct((taps, channels), F32),
            jax.ShapeDtypeStruct((1, channels), F32),
        ),
        in_specs=[in_vmem] + [anywhere] * 3,
        out_specs=(anywhere,) * 3 + (in_vmem,) * 2,
        scratch_shapes=[vmem(3, *shape), pltpu.SemaphoreType.DMA((2, 3, 4))],
    )(small, grad_gate, grad_signal, grad_filter)
    whole = (channels, length)
    return (
        grad_gate.reshape(whole),
        grad_signal.reshape(whole),
        grad_filter.reshape(whole),
        grad_kernel.T,
        grad_skip[0],
    )


def solution(mesh):
    placed = (
        P("chan", "ctx"),
        P("chan", "ctx"),
        P("chan", "ctx"),
        P("chan", None),
        P("chan"),
        P(None, "chan"),
        P("chan", "ctx"),
    )
    return jax.shard_map(
        per_device,
        mesh=mesh,
        in_specs=placed,
        out_specs=(
            P("chan", "ctx"),
            P("chan", "ctx"),
            P("chan", "ctx"),
            P("chan", None),
            P("chan"),
        ),
        check_vma=False,
    )
```
